256 devices in a mesh: feat: 8 (over x, core), rows: 32 (over y, z).
Axes of the slice: x: 4, y: 4, z: 8, core: 2. Of those that a mesh axis runs over, the one named last changes fastest.
Arguments:
- samples: float32 [440, 262144], P(None, ('feat', 'rows')), may hold values from -6 to 6, as said below
- residual: float32 [147, 262144], P(None, ('feat', 'rows')), may hold values from -12 to 12, as said below
- bank: float32 [8, 440, 1024], P(None, None, 'feat'), may hold values from -0.25 to 0.25
- bank_phase: float32 [8, 1024], P(None, 'feat'), may hold values from -3.140625 to 3.140625
- bank_weights: float32 [8, 147, 1024], P(None, None, 'feat'), may hold values from -4 to 4
- block_index: int32 [1], replicated, may hold values from 0 to 7
Outputs:
- new_weights: float32 [147, 1024], P(None, 'feat')
- new_residual: float32 [147, 262144], P(None, ('feat', 'rows'))
The draws below stay inside these ranges and needn't reach their ends.
Inputs may be any that keep to these rules, and one draw needn't show every extreme that they name: `samples`: frames of the input features. `residual`: targets that depend partly on the frames.
All inputs are finite; a program needn't handle non-finite values.
Results may differ from the reference program's by a relative error of at most 0.0003.
Values sent between devices are 32-bit elements; how exact they have to be, the bound alone decides.
No kernel may reach another device: no remote copies, remote signals or barrier semaphores. Data moves between devices by JAX's collectives and lax.ppermute only.
A program may use at most 128 MiB of HBM per device.

```python
import jax
import jax.numpy as jnp
from jax import lax

D = 440
C = 147
FB = 1024
NBLK = 8
ROW_DEV = 1024
NTOT = 262144
N_ROWS = 32


def frames_from(key):
    inner = jax.random.fold_in(key, 7)
    values = jax.random.normal(inner, (D, NTOT), jnp.float32)
    return jnp.clip(values, -6.0, 6.0)


def draw_samples(key, part):
    return frames_from(key)


def draw_residual(key, part):
    frames = frames_from(key)
    mixing = jax.random.normal(jax.random.fold_in(key, 11), (C, D), jnp.float32) * D ** (-0.5)
    noise = jax.random.normal(jax.random.fold_in(key, 13), (C, NTOT), jnp.float32)
    values = jnp.dot(mixing, frames) + 0.5 * noise
    return jnp.clip(values, -12.0, 12.0)


def shard_levels(key, shape, split, smallest, high):
    def one(dim, parts):
        heights = jax.random.uniform(jax.random.fold_in(jax.random.fold_in(key, 6), dim), (parts,), jnp.float32, smallest / len(split), high / len(split))
        return jnp.repeat(jnp.exp(heights), shape[dim] // parts).reshape((-1,) + (1,) * (len(shape) - dim - 1))

    level = one(*split[0])
    for cut in split[1:]:
        level = level * one(*cut)
    return level


def scatter_about(stream_key, dims, scale, most, cuts=(), kind=jnp.bfloat16):
    array = jax.random.normal(stream_key, dims, jnp.float32) * scale
    if len(cuts) > 0:
        array = shard_levels(stream_key, dims, cuts, -0.22, 0.18) * array
    return jnp.clip(array, min=-most, max=most).astype(kind)


def setup_inputs(seed: int = 0) -> dict:
    keys = jax.random.split(jax.random.key(seed), 7)
    samples = draw_samples(jax.random.fold_in(keys[6], 71), 0)
    residual = draw_residual(jax.random.fold_in(keys[6], 71), 0)
    bank = scatter_about(keys[2], (NBLK, D, FB), D ** -0.5, 0.25, ((2, 8),), jnp.float32)
    bank_phase = jnp.clip(jax.random.uniform(keys[3], (NBLK, FB), jnp.float32, -3.140625, 3.140625), -3.140625, 3.140625)
    bank_weights = scatter_about(keys[4], (NBLK, C, FB), 0.5, 4.0, ((2, 8),), jnp.float32)
    block_index = jax.random.randint(keys[5], (1,), 0, NBLK).astype(jnp.int32)
    return {"samples": samples, "residual": residual, "bank": bank, "bank_phase": bank_phase, "bank_weights": bank_weights, "block_index": block_index}


ridge_weight = 0.05

def features_of(projection, phases, block):
    inner = lax.dot_general(projection.astype(jnp.float32), block.astype(jnp.float32), (((0,), (0,)), ((), ())), precision=lax.Precision.HIGHEST, preferred_element_type=jnp.float32)
    return jnp.cos(inner + phases[:, None])

def reference(samples, residual, bank, bank_phase, bank_weights, block_index):
    chosen = block_index[0]
    projection = lax.dynamic_index_in_dim(bank, chosen, 0, keepdims=False)
    phases = lax.dynamic_index_in_dim(bank_phase, chosen, 0, keepdims=False)
    weights = lax.dynamic_index_in_dim(bank_weights, chosen, 0, keepdims=False)
    width = ROW_DEV * N_ROWS
    count = NTOT // width

    def accumulate(index, carry):
        gram, right = carry
        start = (index * width).astype(jnp.int32)
        block = lax.dynamic_slice_in_dim(samples, start, width, 1)
        target = lax.dynamic_slice_in_dim(residual, start, width, 1)
        features = features_of(projection, phases, block)
        gram = gram + lax.dot_general(features.astype(jnp.float32), features.astype(jnp.float32), (((1,), (1,)), ((), ())), precision=lax.Precision.HIGHEST, preferred_element_type=jnp.float32)
        right = right + lax.dot_general(features.astype(jnp.float32), target.astype(jnp.float32), (((1,), (1,)), ((), ())), precision=lax.Precision.HIGHEST, preferred_element_type=jnp.float32)
        return (gram, right)
    start_carry = (jnp.zeros((FB, FB), jnp.float32), jnp.zeros((FB, C), jnp.float32))
    gram, right = lax.fori_loop(0, count, accumulate, start_carry)
    system = gram / NTOT + ridge_weight * jnp.eye(FB, dtype=jnp.float32)
    right = right / NTOT - ridge_weight * weights.T
    factor = jnp.linalg.cholesky(system)
    middle = lax.linalg.triangular_solve(factor, right, left_side=True, lower=True)
    update_block = lax.linalg.triangular_solve(factor, middle, left_side=True, lower=True, transpose_a=True)
    new_weights = weights + update_block.T

    def correct(index, current):
        start = (index * width).astype(jnp.int32)
        block = lax.dynamic_slice_in_dim(samples, start, width, 1)
        target = lax.dynamic_slice_in_dim(current, start, width, 1)
        features = features_of(projection, phases, block)
        fitted = lax.dot_general(update_block.astype(jnp.float32), features.astype(jnp.float32), (((0,), (0,)), ((), ())), precision=lax.Precision.HIGHEST, preferred_element_type=jnp.float32)
        return lax.dynamic_update_slice_in_dim(current, target - fitted, start, 1)
    new_residual = lax.fori_loop(0, count, correct, residual)
    return (new_weights, new_residual)
```

```python
import jax
import jax.numpy as jnp
from jax import lax
from jax.experimental import pallas as pl
from jax.experimental.pallas import tpu as pltpu
from jax.sharding import PartitionSpec as P

ridge_weight = 0.05
D = 440
C = 147
FB = 1024
NB = 8
PAD = 152
COLS = 1024
OFF = [0]
for _k in range(NB):
    OFF.append(OFF[-1] + (NB - _k) * 128 + PAD)
T = OFF[-1]
HALF = T // 2
QUART = T // 8
CHUNK = 24
TURN = 0.15915494309189535
COS = (0.9999999890590223, -19.739204499453898, 64.93911745989527, -85.4501395308797, 60.167630950920234, -25.967599248327534, 6.528658161042403)
f32 = jnp.float32
bf16 = jnp.bfloat16
NN = (((1,), (0,)), ((), ()))
NT = (((1,), (1,)), ((), ()))


def dot(l, r, dims):
    return lax.dot_general(l, r, dims, preferred_element_type=f32)


def split2(x):
    a = x.astype(bf16)
    return a, (x - a.astype(f32)).astype(bf16)


def split3(x):
    a = x.astype(bf16)
    r = x - a.astype(f32)
    b = r.astype(bf16)
    return a, b, (r - b.astype(f32)).astype(bf16)


def gram_kernel(meta, proj, samples, residual, weights, packed, fh, fl):
    s = jnp.concatenate([samples[...], jnp.zeros((8, COLS), f32)], axis=0)
    sh, sl = split2(s)
    for f in range(8):
        turned = (proj[meta[f]] * TURN).T
        h, l = split2(turned)
        y = dot(h, sh, NN) + dot(h, sl, NN) + dot(l, sh, NN) + turned[:, D : D + 1]
        r = y - jnp.round(y)
        z = r * r
        c = jnp.full_like(z, COS[-1])
        for a in COS[-2::-1]:
            c = c * z + a
        ch, cl = split2(c)
        fh[128 * f : 128 * f + 128, :] = ch
        fl[128 * f : 128 * f + 128, :] = cl
    rh, rl = split2(jnp.concatenate([residual[...], jnp.zeros((PAD - C, COLS), f32)], axis=0))
    inv = 1.0 / (COLS * 256)
    ridge = jnp.concatenate([weights[...], jnp.zeros((PAD - C, 128), f32)], axis=0) * (-ridge_weight)
    for q in range(4):
        o = 256 * q
        ch, cl = fh[o : o + 256, :], fl[o : o + 256, :]
        g = (dot(fh[o:, :], ch, NT) + dot(fh[o:, :], cl, NT) + dot(fl[o:, :], ch, NT)) * inv
        r = (dot(rh, ch, NT) + dot(rh, cl, NT) + dot(rl, ch, NT)) * inv
        for j in range(2):
            k = 2 * q + j
            m = (NB - k) * 128
            packed[OFF[k] : OFF[k] + m, :] = g[128 * j :, 128 * j : 128 * j + 128]
            own = jnp.where(meta[8] == k, 1.0, 0.0)
            packed[OFF[k] + m : OFF[k] + m + PAD, :] = r[:, 128 * j : 128 * j + 128] + ridge * own


def invert_block(rows, lane, sub):
    d = list(rows)
    for g in range(16):
        c0 = 8 * g
        top = d[g]
        cb = [jnp.broadcast_to(top[:, c0 + j : c0 + j + 1], (8, 128)) for j in range(8)]
        t = {}
        for j in range(8):
            for i in range(j, 8):
                t[i, j] = jnp.broadcast_to(cb[j][i : i + 1, :], (8, 128))
        for j in range(8):
            inv = 1.0 / t[j, j]
            col = {i: (t[i, j] if i > j else t[j, i]) for i in range(8) if i != j}
            scaled = {i: col[i] * inv for i in col}
            for i in range(8):
                if i == j:
                    continue
                for k in range(i + 1):
                    if k != j:
                        t[i, k] = t[i, k] - scaled[i] * col[k]
            for i in col:
                t[max(i, j), min(i, j)] = scaled[i]
            t[j, j] = -inv

        def column(j):
            e = [t[max(i, j), min(i, j)] for i in range(8)]
            odd = (sub & 1) == 0
            e = [jnp.where(odd, e[2 * i], e[2 * i + 1]) for i in range(4)]
            two = (sub & 2) == 0
            e = [jnp.where(two, e[0], e[1]), jnp.where(two, e[2], e[3])]
            return jnp.where(sub < 4, e[0], e[1])

        pivot = [column(j) for j in range(8)]
        inside = (lane >= c0) & (lane < c0 + 8)
        unit = jnp.where(inside, jnp.where(lane - c0 == sub, 1.0, 0.0), top)
        new = pivot[0] * jnp.broadcast_to(unit[0:1, :], (8, 128))
        for j in range(1, 8):
            new = new + pivot[j] * jnp.broadcast_to(unit[j : j + 1, :], (8, 128))
        spread = [jnp.broadcast_to(new[j : j + 1, :], (8, 128)) for j in range(8)]
        for i in list(range(g + 1, 16)) + list(range(g)):
            acc = jnp.where(inside, 0.0, d[i])
            for j in range(8):
                acc = acc + jnp.broadcast_to(d[i][:, c0 + j : c0 + j + 1], (8, 128)) * spread[j]
            d[i] = acc
        d[g] = -new
    return d


def stack_left(x):
    a, b, c = split3(x)
    return jnp.concatenate([a, a, b, a, c, b], axis=1)


def stack_right(x):
    a, b, c = split3(x)
    return jnp.concatenate([a, b, a, c, a, b], axis=1)


def solve_kernel(meta, own, other, fh_in, fl_in, residual, weights, new_weights, new_residual, p, dinv, us, fh, fl, sem, fsem):
    x, core = meta[0], meta[1]
    pieces = []
    for side, src in enumerate((own, other)):
        half = core if side == 0 else 1 - core
        for s in range(4):
            row = half * HALF + ((x + 4 - s) % 4) * QUART
            row = pl.multiple_of(row, 8)
            pieces.append(pltpu.make_async_copy(src.at[s], p.at[pl.ds(row, QUART)], sem))
    later = [pltpu.make_async_copy(fh_in, fh, fsem), pltpu.make_async_copy(fl_in, fl, fsem)]
    for c in pieces + later:
        c.start()
    for c in pieces:
        c.wait()
    lane = lax.broadcasted_iota(jnp.int32, (8, 128), 1)
    sub = lax.broadcasted_iota(jnp.int32, (8, 128), 0)
    for k in range(NB):
        o = OFF[k]
        rows = [
            p[o + 8 * g : o + 8 * g + 8, :] + jnp.where(lane == 8 * g + sub, ridge_weight, 0.0)
            for g in range(16)
        ]
        rows = invert_block(rows, lane, sub)
        for g in range(16):
            dinv[8 * g : 8 * g + 8, :] = rows[g]
        m = (NB - 1 - k) * 128 + PAD
        below = p[o + 128 : o + 128 + m, :]
        gain = dot(stack_left(below), stack_right(dinv[...]), NT)
        if k < NB - 1:
            left = stack_left(gain)
            right = stack_right(below[: m - PAD])
            for j in range(k + 1, NB):
                b = (j - k - 1) * 128
                at = OFF[j]
                p[at : at + m - b, :] = p[at : at + m - b, :] - dot(left[b:], right[b : b + 128], NT)
        p[o + 128 : o + 128 + m, :] = gain
    u = [None] * NB
    for k in reversed(range(NB)):
        o = OFF[k]
        m = (NB - 1 - k) * 128
        acc = p[o + 128 + m : o + 128 + m + PAD, :]
        if k < NB - 1:
            done = jnp.concatenate(u[k + 1 :], axis=1)
            acc = acc - lax.dot_general(
                done,
                p[o + 128 : o + 128 + m, :],
                NN,
                precision=lax.Precision.HIGHEST,
                preferred_element_type=f32,
            )
        u[k] = acc
        us[k] = acc
    full = jnp.concatenate(u, axis=1)
    uh, ul = split2(full)
    new_weights[...] = weights[...] + us[2 * x + core][:C]
    for c in later:
        c.wait()
    fit = dot(uh, fh[...], NN) + dot(uh, fl[...], NN) + dot(ul, fh[...], NN)
    new_residual[...] = residual[...] - fit[:C]


def x_perm(s):
    return [(f, ((f // 2 + s) % 4) * 2 + f % 2) for f in range(8)]


core_swap = [(f, f ^ 1) for f in range(8)]


def per_device(samples, residual, bank, bank_phase, bank_weights, block_index):
    chosen = block_index[0]
    feat = lax.axis_index("feat")
    rows = lax.axis_index("rows")
    x, core = feat // 2, feat % 2
    block = jnp.concatenate(
        [
            lax.dynamic_index_in_dim(bank, chosen, 0, keepdims=False),
            lax.dynamic_index_in_dim(bank_phase, chosen, 0, keepdims=True),
            jnp.zeros((7, 128), f32),
        ],
        axis=0,
    )
    local_weights = lax.dynamic_index_in_dim(bank_weights, chosen, 0, keepdims=False)
    mine = jnp.stack([block] + [lax.ppermute(block, "feat", x_perm(s)) for s in (1, 2, 3)])
    theirs = lax.ppermute(mine, "feat", core_swap)
    proj = jnp.concatenate([mine, theirs], axis=0)
    order = [
        (x + 4 - f // 2) % 4 + jnp.where(core == f % 2, 0, 4) for f in range(8)
    ]
    meta = jnp.stack(order + [jnp.where(rows == 0, feat, -1)]).astype(jnp.int32)
    smem = pl.BlockSpec(memory_space=pltpu.SMEM)
    vmem = pl.BlockSpec(memory_space=pltpu.VMEM)
    hbm = pl.BlockSpec(memory_space=pl.ANY)
    packed, fh, fl = pl.pallas_call(
        gram_kernel,
        out_shape=(
            jax.ShapeDtypeStruct((T, 128), f32),
            jax.ShapeDtypeStruct((FB, COLS), bf16),
            jax.ShapeDtypeStruct((FB, COLS), bf16),
        ),
        in_specs=[smem, vmem, vmem, vmem, vmem],
        out_specs=(vmem, vmem, vmem),
        compiler_params=pltpu.CompilerParams(vmem_limit_bytes=56 << 20),
        name="features_gram",
    )(meta, proj, samples, residual, local_weights)

    halves = packed.reshape(2, HALF, 128)
    keep = lax.dynamic_index_in_dim(halves, core, 0, keepdims=False)
    give = lax.dynamic_index_in_dim(halves, 1 - core, 0, keepdims=False)
    half = keep + lax.ppermute(give, "feat", core_swap)
    quarters = half.reshape(4, QUART, 128)
    got = [
        lax.ppermute(
            lax.dynamic_index_in_dim(quarters, (x + s) % 4, 0, keepdims=False), "feat", x_perm(s)
        )
        for s in (1, 2, 3)
    ]
    quarter = lax.dynamic_index_in_dim(quarters, x, 0, keepdims=False) + got[0] + got[1] + got[2]
    spread = jnp.pad(quarter, ((0, 32 * CHUNK - QUART), (0, 0))).reshape(32, CHUNK, 128)
    chunk = jnp.sum(lax.all_to_all(spread, "rows", 0, 0), axis=0)
    full = lax.all_to_all(jnp.broadcast_to(chunk[None], (32, CHUNK, 128)), "rows", 0, 0)
    quarter = full.reshape(32 * CHUNK, 128)[:QUART]
    own = jnp.stack([quarter] + [lax.ppermute(quarter, "feat", x_perm(s)) for s in (1, 2, 3)])
    other = lax.ppermute(own, "feat", core_swap)

    where = jnp.stack([x, core]).astype(jnp.int32)
    new_weights, new_residual = pl.pallas_call(
        solve_kernel,
        out_shape=(
            jax.ShapeDtypeStruct((C, 128), f32),
            jax.ShapeDtypeStruct((C, COLS), f32),
        ),
        in_specs=[smem, hbm, hbm, hbm, hbm, vmem, vmem],
        out_specs=(vmem, vmem),
        scratch_shapes=[
            pltpu.VMEM((T, 128), f32),
            pltpu.VMEM((128, 128), f32),
            pltpu.VMEM((NB, PAD, 128), f32),
            pltpu.VMEM((FB, COLS), bf16),
            pltpu.VMEM((FB, COLS), bf16),
            pltpu.SemaphoreType.DMA,
            pltpu.SemaphoreType.DMA,
        ],
        compiler_params=pltpu.CompilerParams(vmem_limit_bytes=56 << 20),
        name="block_solve",
    )(where, own, other, fh, fl, residual, local_weights)
    return (new_weights, new_residual)


def solution(mesh):
    in_specs = (
        P(None, ("feat", "rows")),
        P(None, ("feat", "rows")),
        P(None, None, "feat"),
        P(None, "feat"),
        P(None, None, "feat"),
        P(),
    )
    out_specs = (P(None, "feat"), P(None, ("feat", "rows")))
    return jax.shard_map(
        per_device, mesh=mesh, in_specs=in_specs, out_specs=out_specs, check_vma=False
    )
```

```python
import jax
import jax.numpy as jnp
from jax import lax
from jax.experimental import pallas as pl
from jax.experimental.pallas import tpu as pltpu
from jax.sharding import PartitionSpec as P

ridge_weight = 0.05
D = 440
C = 147
FB = 1024
NB = 8
PAD = 152
COLS = 1024
OFF = [0]
for _k in range(NB):
    OFF.append(OFF[-1] + (NB - _k) * 128 + PAD)
T = OFF[-1]
HALF = T // 2
QUART = T // 8
CHUNK = 24
TURN = 0.15915494309189535
COS = (0.9999999890590223, -19.739204499453898, 64.93911745989527, -85.4501395308797, 60.167630950920234, -25.967599248327534, 6.528658161042403)
f32 = jnp.float32
bf16 = jnp.bfloat16
NN = (((1,), (0,)), ((), ()))
NT = (((1,), (1,)), ((), ()))


def dot(l, r, dims):
    return lax.dot_general(l, r, dims, preferred_element_type=f32)


def split2(x):
    a = x.astype(bf16)
    return a, (x - a.astype(f32)).astype(bf16)


def split3(x):
    a = x.astype(bf16)
    r = x - a.astype(f32)
    b = r.astype(bf16)
    return a, b, (r - b.astype(f32)).astype(bf16)


def gram_kernel(meta, proj, samples, residual, weights, packed, fh, fl):
    s = jnp.concatenate([samples[...], jnp.zeros((8, COLS), f32)], axis=0)
    sh, sl = split2(s)
    for f in range(8):
        turned = (proj[meta[f]] * TURN).T
        h, l = split2(turned)
        y = dot(h, sh, NN) + dot(h, sl, NN) + dot(l, sh, NN) + turned[:, D : D + 1]
        r = y - jnp.round(y)
        z = r * r
        c = jnp.full_like(z, COS[-1])
        for a in COS[-2::-1]:
            c = c * z + a
        ch, cl = split2(c)
        fh[128 * f : 128 * f + 128, :] = ch
        fl[128 * f : 128 * f + 128, :] = cl
    rh, rl = split2(jnp.concatenate([residual[...], jnp.zeros((PAD - C, COLS), f32)], axis=0))
    inv = 1.0 / (COLS * 256)

    def put(at, value):
        n = value.shape[0]
        low = min(max(HALF - at, 0), n)
        if low > 0:
            packed[meta[9], at : at + low, :] = value[:low]
        if low < n:
            packed[1 - meta[9], at + low - HALF : at + n - HALF, :] = value[low:]

    ridge = jnp.concatenate([weights[...], jnp.zeros((PAD - C, 128), f32)], axis=0) * (-ridge_weight)
    for q in range(4):
        o = 256 * q
        ch, cl = fh[o : o + 256, :], fl[o : o + 256, :]
        g = (dot(fh[o:, :], ch, NT) + dot(fh[o:, :], cl, NT) + dot(fl[o:, :], ch, NT)) * inv
        r = (dot(rh, ch, NT) + dot(rh, cl, NT) + dot(rl, ch, NT)) * inv
        for j in range(2):
            k = 2 * q + j
            m = (NB - k) * 128
            put(OFF[k], g[128 * j :, 128 * j : 128 * j + 128])
            own = jnp.where(meta[8] == k, 1.0, 0.0)
            put(OFF[k] + m, r[:, 128 * j : 128 * j + 128] + ridge * own)


def tree(xs):
    xs = list(xs)
    while len(xs) > 1:
        last = [xs[-1]] if len(xs) % 2 else []
        xs = [xs[i] + xs[i + 1] for i in range(0, len(xs) - 1, 2)] + last
    return xs[0]


def sweep_slab(rows, lane, sub):
    d = list(rows)
    n = len(d)
    for g in range(n):
        c0 = 8 * g
        top = d[g]
        t = {}
        for j in range(8):
            cj = jnp.broadcast_to(top[:, c0 + j : c0 + j + 1], (8, 128))
            for i in range(j, 8):
                t[i, j] = jnp.take_along_axis(cj, jnp.full((8, 128), i, jnp.int32), axis=0)
        for p in range(0, 8, 2):
            q = p + 1
            e = 1.0 / (t[p, p] * t[q, q] - t[q, p] * t[q, p])
            epp, eqq, eqp = t[q, q] * e, t[p, p] * e, t[q, p] * e
            rest = [i for i in range(8) if i not in (p, q)]
            cp = {i: t[max(i, p), min(i, p)] for i in rest}
            cq = {i: t[max(i, q), min(i, q)] for i in rest}
            lp = {i: (cp[i] * t[q, q] - cq[i] * t[q, p]) * e for i in rest}
            lq = {i: (cq[i] * t[p, p] - cp[i] * t[q, p]) * e for i in rest}
            for i in rest:
                for k in rest:
                    if k <= i:
                        t[i, k] = t[i, k] - (lp[i] * cp[k] + lq[i] * cq[k])
            for i in rest:
                t[max(i, p), min(i, p)] = lp[i]
                t[max(i, q), min(i, q)] = lq[i]
            t[p, p], t[q, q], t[q, p] = -epp, -eqq, eqp

        def column(j):
            e = [t[max(i, j), min(i, j)] for i in range(8)]
            even = (sub & 1) == 0
            e = [jnp.where(even, e[2 * i], e[2 * i + 1]) for i in range(4)]
            low = (sub & 2) == 0
            e = [jnp.where(low, e[0], e[1]), jnp.where(low, e[2], e[3])]
            return jnp.where(sub < 4, e[0], e[1])

        inside = (lane >= c0) & (lane < c0 + 8)
        unit = [
            jnp.where(
                inside,
                jnp.where(lane == c0 + j, 1.0, 0.0),
                jnp.broadcast_to(top[j : j + 1, :], (8, 128)),
            )
            for j in range(8)
        ]
        new = tree([column(j) * unit[j] for j in range(8)])
        spread = [jnp.broadcast_to(new[j : j + 1, :], (8, 128)) for j in range(8)]
        for i in list(range(g + 1, n)) + list(range(g)):
            old = d[i]
            d[i] = jnp.where(inside, 0.0, old) + tree(
                [jnp.broadcast_to(old[:, c0 + j : c0 + j + 1], (8, 128)) * spread[j] for j in range(8)]
            )
        d[g] = -new
    return d


def invert_block(d, lane, sub):
    wide = lax.broadcasted_iota(jnp.int32, (64, 128), 1)

    def body(s, carry):
        slab = sweep_slab([d[8 * i : 8 * i + 8, :] for i in range(8)], lane, sub)
        slab = jnp.concatenate(slab, axis=0)
        a, b, c = split3(jnp.concatenate([slab, jnp.zeros((64, 128), f32)], axis=0))
        rest = d[64:, :]
        rest = jnp.where(wide < 64, 0.0, rest) - dot(
            stack_left(rest), jnp.concatenate([a, b, a, c, a, b], axis=0), NN
        )
        d[:64, :] = pltpu.roll(rest, 64, 1)
        d[64:, :] = pltpu.roll(slab, 64, 1)
        return carry

    lax.fori_loop(0, 2, body, 0)


def stack_left(x):
    a, b, c = split3(x)
    return jnp.concatenate([a, a, b, a, c, b], axis=1)


def stack_right(x):
    a, b, c = split3(x)
    return jnp.concatenate([a, b, a, c, a, b], axis=1)


def solve_kernel(meta, own, other, fh_in, fl_in, residual, weights, new_weights, new_residual, p, dinv, us, fh, fl, sem, fsem):
    core = meta[1]
    pieces = []
    for side, src in enumerate((own, other)):
        half = core if side == 0 else 1 - core
        for s in range(4):
            row = half * HALF + ((meta[2 + side] + 4 - s) % 4) * QUART
            row = pl.multiple_of(row, 8)
            pieces.append(pltpu.make_async_copy(src.at[s], p.at[pl.ds(row, QUART)], sem))
    later = [pltpu.make_async_copy(fh_in, fh, fsem), pltpu.make_async_copy(fl_in, fl, fsem)]
    for c in pieces + later:
        c.start()
    for c in pieces:
        c.wait()
    lane = lax.broadcasted_iota(jnp.int32, (8, 128), 1)
    sub = lax.broadcasted_iota(jnp.int32, (8, 128), 0)
    eye = jnp.where(
        lax.broadcasted_iota(jnp.int32, (128, 128), 0) == lax.broadcasted_iota(jnp.int32, (128, 128), 1),
        ridge_weight,
        0.0,
    )
    def panel(k, carry):
        o = pl.multiple_of(k * (FB + PAD) - 64 * k * (k - 1), 8)
        dinv[...] = p[pl.ds(o, 128), :] + eye
        invert_block(dinv, lane, sub)
        for which in range(NB):
            pl.when(k == which)(lambda which=which: trailing(which))
        return carry

    def trailing(k):
        o = OFF[k]
        m = (NB - 1 - k) * 128 + PAD
        below = p[o + 128 : o + 128 + m, :]
        gain = dot(stack_left(below), stack_right(dinv[...]), NT)
        if k < NB - 1:
            left = stack_left(gain)
            right = stack_right(below[: m - PAD])
            j = k + 1
            if (NB - j) % 2:
                p[OFF[j] : OFF[j] + m, :] = p[OFF[j] : OFF[j] + m, :] - dot(left, right[:128], NT)
                j += 1
            while j < NB:
                b = (j - k - 1) * 128
                n = m - b
                both = dot(left[b:], right[b : b + 256], NT)
                p[OFF[j] : OFF[j] + n, :] = p[OFF[j] : OFF[j] + n, :] - both[:, :128]
                n -= 128
                p[OFF[j + 1] : OFF[j + 1] + n, :] = p[OFF[j + 1] : OFF[j + 1] + n, :] - both[128:, 128:]
                j += 2
        p[o + 128 : o + 128 + m, :] = gain

    lax.fori_loop(0, NB, panel, 0)
    u = [None] * NB
    for k in reversed(range(NB)):
        o = OFF[k]
        m = (NB - 1 - k) * 128
        acc = p[o + 128 + m : o + 128 + m + PAD, :]
        if k < NB - 1:
            done = jnp.concatenate(u[k + 1 :], axis=1)
            acc = acc - lax.dot_general(
                done,
                p[o + 128 : o + 128 + m, :],
                NN,
                precision=lax.Precision.HIGHEST,
                preferred_element_type=f32,
            )
        u[k] = acc
        us[k] = acc
    full = jnp.concatenate(u, axis=1)
    uh, ul = split2(full)
    new_weights[...] = weights[...] + us[meta[0]][:C]
    for c in later:
        c.wait()
    fit = dot(uh, fh[...], NN) + dot(uh, fl[...], NN) + dot(ul, fh[...], NN)
    new_residual[...] = residual[...] - fit[:C]


def x_perm(s):
    return [(f, ((f // 2 + s) % 4) * 2 + f % 2) for f in range(8)]


BOTH = ("feat", "rows")


def device_of(x, y, z, c):
    return (2 * x + c) * 32 + 8 * y + z


def ring_perm(s):
    pairs = []
    for x in range(4):
        for y in range(4):
            for z in range(8):
                pairs.append((device_of(x, y, z, 0), device_of((x + s) % 4, y, z, 0)))
                pairs.append((device_of(x, y, z, 1), device_of(x, (y + s) % 4, z, 1)))
    return pairs


GROUPS = [[device_of(x, y, z, 0) for y in range(4) for z in range(8)] for x in range(4)] + [
    [device_of(x, y, z, 1) for x in range(4) for z in range(8)] for y in range(4)
]

core_swap = [(f, f ^ 1) for f in range(8)]


def per_device(samples, residual, bank, bank_phase, bank_weights, block_index):
    chosen = block_index[0]
    feat = lax.axis_index("feat")
    rows = lax.axis_index("rows")
    x, core = feat // 2, feat % 2
    y = rows // 8
    block = jnp.concatenate(
        [
            lax.dynamic_index_in_dim(bank, chosen, 0, keepdims=False),
            lax.dynamic_index_in_dim(bank_phase, chosen, 0, keepdims=True),
            jnp.zeros((7, 128), f32),
        ],
        axis=0,
    )
    local_weights = lax.dynamic_index_in_dim(bank_weights, chosen, 0, keepdims=False)
    mine = jnp.stack([block] + [lax.ppermute(block, "feat", x_perm(s)) for s in (1, 2, 3)])
    theirs = lax.ppermute(mine, "feat", core_swap)
    proj = jnp.concatenate([mine, theirs], axis=0)
    order = [
        (x + 4 - f // 2) % 4 + jnp.where(core == f % 2, 0, 4) for f in range(8)
    ]
    meta = jnp.stack(order + [jnp.where(rows == 0, feat, -1), core]).astype(jnp.int32)
    smem = pl.BlockSpec(memory_space=pltpu.SMEM)
    vmem = pl.BlockSpec(memory_space=pltpu.VMEM)
    hbm = pl.BlockSpec(memory_space=pl.ANY)
    packed, fh, fl = pl.pallas_call(
        gram_kernel,
        out_shape=(
            jax.ShapeDtypeStruct((2, HALF, 128), f32),
            jax.ShapeDtypeStruct((FB, COLS), bf16),
            jax.ShapeDtypeStruct((FB, COLS), bf16),
        ),
        in_specs=[smem, vmem, vmem, vmem, vmem],
        out_specs=(vmem, vmem, vmem),
        compiler_params=pltpu.CompilerParams(vmem_limit_bytes=56 << 20),
        name="features_gram",
    )(meta, proj, samples, residual, local_weights)

    spot = jnp.where(core == 0, x, y)
    half = packed[0] + lax.ppermute(packed[1], "feat", core_swap)
    quarters = half.reshape(4, QUART, 128)
    got = [
        lax.ppermute(
            lax.dynamic_index_in_dim(quarters, (spot + s) % 4, 0, keepdims=False), BOTH, ring_perm(s)
        )
        for s in (1, 2, 3)
    ]
    quarter = lax.dynamic_index_in_dim(quarters, spot, 0, keepdims=False) + got[0] + got[1] + got[2]
    spread = jnp.pad(quarter, ((0, 32 * CHUNK - QUART), (0, 0))).reshape(32, CHUNK, 128)
    chunk = jnp.sum(lax.all_to_all(spread, BOTH, 0, 0, axis_index_groups=GROUPS), axis=0)
    full = lax.all_to_all(
        jnp.broadcast_to(chunk[None], (32, CHUNK, 128)), BOTH, 0, 0, axis_index_groups=GROUPS
    )
    quarter = full.reshape(32 * CHUNK, 128)[:QUART]
    own = jnp.stack([quarter] + [lax.ppermute(quarter, BOTH, ring_perm(s)) for s in (1, 2, 3)])
    other = lax.ppermute(own, "feat", core_swap)

    where = jnp.stack([feat, core, spot, jnp.where(core == 0, y, x)]).astype(jnp.int32)
    new_weights, new_residual = pl.pallas_call(
        solve_kernel,
        out_shape=(
            jax.ShapeDtypeStruct((C, 128), f32),
            jax.ShapeDtypeStruct((C, COLS), f32),
        ),
        in_specs=[smem, hbm, hbm, hbm, hbm, vmem, vmem],
        out_specs=(vmem, vmem),
        scratch_shapes=[
            pltpu.VMEM((T, 128), f32),
            pltpu.VMEM((128, 128), f32),
            pltpu.VMEM((NB, PAD, 128), f32),
            pltpu.VMEM((FB, COLS), bf16),
            pltpu.VMEM((FB, COLS), bf16),
            pltpu.SemaphoreType.DMA,
            pltpu.SemaphoreType.DMA,
        ],
        compiler_params=pltpu.CompilerParams(vmem_limit_bytes=56 << 20),
        name="block_solve",
    )(where, own, other, fh, fl, residual, local_weights)
    return (new_weights, new_residual)


def solution(mesh):
    in_specs = (
        P(None, ("feat", "rows")),
        P(None, ("feat", "rows")),
        P(None, None, "feat"),
        P(None, "feat"),
        P(None, None, "feat"),
        P(),
    )
    out_specs = (P(None, "feat"), P(None, ("feat", "rows")))
    return jax.shard_map(
        per_device, mesh=mesh, in_specs=in_specs, out_specs=out_specs, check_vma=False
    )
```

```python
import jax
import jax.numpy as jnp
from jax import lax
from jax.experimental import pallas as pl
from jax.experimental.pallas import tpu as pltpu
from jax.sharding import PartitionSpec as P

ridge_weight = 0.05
D = 440
C = 147
FB = 1024
NB = 8
PAD = 152
COLS = 1024
OFF = [0]
for _k in range(NB):
    OFF.append(OFF[-1] + (NB - _k) * 128 + PAD)
T = OFF[-1]
HALF = T // 2
QUART = T // 8
CHUNK = 24
TURN = 0.15915494309189535
COS = (0.9999999890590223, -19.739204499453898, 64.93911745989527, -85.4501395308797, 60.167630950920234, -25.967599248327534, 6.528658161042403)
f32 = jnp.float32
bf16 = jnp.bfloat16
NN = (((1,), (0,)), ((), ()))
NT = (((1,), (1,)), ((), ()))


def dot(l, r, dims):
    return lax.dot_general(l, r, dims, preferred_element_type=f32)


def split2(x):
    a = x.astype(bf16)
    return a, (x - a.astype(f32)).astype(bf16)


def split3(x):
    a = x.astype(bf16)
    r = x - a.astype(f32)
    b = r.astype(bf16)
    return a, b, (r - b.astype(f32)).astype(bf16)


def gram_kernel(
    meta, mine, theirs, samples_in, residual_in, weights_in, keep, give, fh_out, fl_out,
    proj, samples, residual, weights, packed, fh, fl, sem,
):
    first = pltpu.make_async_copy(samples_in, samples, sem.at[0])
    blocks = [
        pltpu.make_async_copy(mine, proj.at[0:4], sem.at[1]),
        pltpu.make_async_copy(theirs, proj.at[4:8], sem.at[2]),
    ]
    rest = [
        pltpu.make_async_copy(residual_in, residual, sem.at[3]),
        pltpu.make_async_copy(weights_in, weights, sem.at[4]),
    ]
    for c in [first] + blocks + rest:
        c.start()
    first.wait()
    s = jnp.concatenate([samples[...], jnp.zeros((8, COLS), f32)], axis=0)
    sh, sl = split2(s)
    for c in blocks:
        c.wait()
    for f in range(8):
        turned = (proj[meta[f]] * TURN).T
        h, l = split2(turned)
        y = dot(h, sh, NN) + dot(h, sl, NN) + dot(l, sh, NN) + turned[:, D : D + 1]
        r = y - jnp.round(y)
        z = r * r
        c = jnp.full_like(z, COS[-1])
        for a in COS[-2::-1]:
            c = c * z + a
        ch, cl = split2(c)
        fh[128 * f : 128 * f + 128, :] = ch
        fl[128 * f : 128 * f + 128, :] = cl
    out = [
        pltpu.make_async_copy(fh, fh_out, sem.at[0]),
        pltpu.make_async_copy(fl, fl_out, sem.at[1]),
    ]
    for c in out:
        c.start()
    for c in rest:
        c.wait()
    rh, rl = split2(jnp.concatenate([residual[...], jnp.zeros((PAD - C, COLS), f32)], axis=0))
    inv = 1.0 / (COLS * 256)

    def put(at, value):
        n = value.shape[0]
        low = min(max(HALF - at, 0), n)
        if low > 0:
            packed[meta[9], at : at + low, :] = value[:low]
        if low < n:
            packed[1 - meta[9], at + low - HALF : at + n - HALF, :] = value[low:]

    ridge = jnp.concatenate([weights[...], jnp.zeros((PAD - C, 128), f32)], axis=0) * (-ridge_weight)
    for q in range(4):
        o = 256 * q
        ch, cl = fh[o : o + 256, :], fl[o : o + 256, :]
        g = (dot(fh[o:, :], ch, NT) + dot(fh[o:, :], cl, NT) + dot(fl[o:, :], ch, NT)) * inv
        r = (dot(rh, ch, NT) + dot(rh, cl, NT) + dot(rl, ch, NT)) * inv
        for j in range(2):
            k = 2 * q + j
            m = (NB - k) * 128
            put(OFF[k], g[128 * j :, 128 * j : 128 * j + 128])
            own = jnp.where(meta[8] == k, 1.0, 0.0)
            put(OFF[k] + m, r[:, 128 * j : 128 * j + 128] + ridge * own)
    out = out + [
        pltpu.make_async_copy(packed.at[1], give, sem.at[2]),
        pltpu.make_async_copy(packed.at[0], keep, sem.at[3]),
    ]
    for c in out[2:]:
        c.start()
    for c in out:
        c.wait()


def tree(xs):
    xs = list(xs)
    while len(xs) > 1:
        last = [xs[-1]] if len(xs) % 2 else []
        xs = [xs[i] + xs[i + 1] for i in range(0, len(xs) - 1, 2)] + last
    return xs[0]


def sweep_slab(rows, lane, sub):
    d = list(rows)
    n = len(d)
    for g in range(n):
        c0 = 8 * g
        top = d[g]
        t = {}
        for j in range(8):
            cj = jnp.broadcast_to(top[:, c0 + j : c0 + j + 1], (8, 128))
            for i in range(j, 8):
                t[i, j] = jnp.take_along_axis(cj, jnp.full((8, 128), i, jnp.int32), axis=0)
        for p in range(0, 8, 2):
            q = p + 1
            e = 1.0 / (t[p, p] * t[q, q] - t[q, p] * t[q, p])
            epp, eqq, eqp = t[q, q] * e, t[p, p] * e, t[q, p] * e
            rest = [i for i in range(8) if i not in (p, q)]
            cp = {i: t[max(i, p), min(i, p)] for i in rest}
            cq = {i: t[max(i, q), min(i, q)] for i in rest}
            lp = {i: (cp[i] * t[q, q] - cq[i] * t[q, p]) * e for i in rest}
            lq = {i: (cq[i] * t[p, p] - cp[i] * t[q, p]) * e for i in rest}
            for i in rest:
                for k in rest:
                    if k <= i:
                        t[i, k] = t[i, k] - (lp[i] * cp[k] + lq[i] * cq[k])
            for i in rest:
                t[max(i, p), min(i, p)] = lp[i]
                t[max(i, q), min(i, q)] = lq[i]
            t[p, p], t[q, q], t[q, p] = -epp, -eqq, eqp

        def column(j):
            e = [t[max(i, j), min(i, j)] for i in range(8)]
            even = (sub & 1) == 0
            e = [jnp.where(even, e[2 * i], e[2 * i + 1]) for i in range(4)]
            low = (sub & 2) == 0
            e = [jnp.where(low, e[0], e[1]), jnp.where(low, e[2], e[3])]
            return jnp.where(sub < 4, e[0], e[1])

        inside = (lane >= c0) & (lane < c0 + 8)
        unit = [
            jnp.where(
                inside,
                jnp.where(lane == c0 + j, 1.0, 0.0),
                jnp.broadcast_to(top[j : j + 1, :], (8, 128)),
            )
            for j in range(8)
        ]
        new = tree([column(j) * unit[j] for j in range(8)])
        spread = [jnp.broadcast_to(new[j : j + 1, :], (8, 128)) for j in range(8)]
        for i in list(range(g + 1, n)) + list(range(g)):
            old = d[i]
            d[i] = jnp.where(inside, 0.0, old) + tree(
                [jnp.broadcast_to(old[:, c0 + j : c0 + j + 1], (8, 128)) * spread[j] for j in range(8)]
            )
        d[g] = -new
    return d


def invert_block(d, lane, sub):
    wide = lax.broadcasted_iota(jnp.int32, (64, 128), 1)

    def body(s, carry):
        slab = sweep_slab([d[8 * i : 8 * i + 8, :] for i in range(8)], lane, sub)
        slab = jnp.concatenate(slab, axis=0)
        a, b, c = split3(jnp.concatenate([slab, jnp.zeros((64, 128), f32)], axis=0))
        rest = d[64:, :]
        rest = jnp.where(wide < 64, 0.0, rest) - dot(
            stack_left(rest), jnp.concatenate([a, b, a, c, a, b], axis=0), NN
        )
        d[:64, :] = pltpu.roll(rest, 64, 1)
        d[64:, :] = pltpu.roll(slab, 64, 1)
        return carry

    lax.fori_loop(0, 2, body, 0)


def stack_left(x):
    a, b, c = split3(x)
    return jnp.concatenate([a, a, b, a, c, b], axis=1)


def stack_right(x):
    a, b, c = split3(x)
    return jnp.concatenate([a, b, a, c, a, b], axis=1)


def solve_kernel(meta, own, other, fh_in, fl_in, residual, weights, new_weights, new_residual, p, dinv, us, fh, fl, sem, fsem):
    core = meta[1]
    pieces = []
    for side, src in enumerate((own, other)):
        half = core if side == 0 else 1 - core
        for s in range(4):
            row = half * HALF + ((meta[2 + side] + 4 - s) % 4) * QUART
            row = pl.multiple_of(row, 8)
            pieces.append(pltpu.make_async_copy(src.at[s], p.at[pl.ds(row, QUART)], sem))
    later = [pltpu.make_async_copy(fh_in, fh, fsem), pltpu.make_async_copy(fl_in, fl, fsem)]
    for c in pieces + later:
        c.start()
    for c in pieces:
        c.wait()
    lane = lax.broadcasted_iota(jnp.int32, (8, 128), 1)
    sub = lax.broadcasted_iota(jnp.int32, (8, 128), 0)
    eye = jnp.where(
        lax.broadcasted_iota(jnp.int32, (128, 128), 0) == lax.broadcasted_iota(jnp.int32, (128, 128), 1),
        ridge_weight,
        0.0,
    )
    def panel(k, carry):
        o = pl.multiple_of(k * (FB + PAD) - 64 * k * (k - 1), 8)
        dinv[...] = p[pl.ds(o, 128), :] + eye
        invert_block(dinv, lane, sub)
        for which in range(NB):
            pl.when(k == which)(lambda which=which: trailing(which))
        return carry

    def trailing(k):
        o = OFF[k]
        m = (NB - 1 - k) * 128 + PAD
        below = p[o + 128 : o + 128 + m, :]
        a, b, c = split3(below)
        da, db, dc = split3(dinv[...])
        zero = jnp.zeros((128, 128), bf16)
        wide = jnp.concatenate(
            [
                jnp.concatenate([da, da, da, zero], axis=1),
                jnp.concatenate([db, db, zero, dc], axis=1),
            ],
            axis=0,
        )
        gain = dot(jnp.concatenate([a, b, c, a], axis=1), wide, NT)
        gain = gain[:, :128] + gain[:, 128:]
        if k < NB - 1:
            left = stack_left(gain)
            right = stack_right(below[: m - PAD])
            j = k + 1
            if (NB - j) % 2:
                p[OFF[j] : OFF[j] + m, :] = p[OFF[j] : OFF[j] + m, :] - dot(left, right[:128], NT)
                j += 1
            while j < NB:
                b = (j - k - 1) * 128
                n = m - b
                both = dot(left[b:], right[b : b + 256], NT)
                p[OFF[j] : OFF[j] + n, :] = p[OFF[j] : OFF[j] + n, :] - both[:, :128]
                n -= 128
                p[OFF[j + 1] : OFF[j + 1] + n, :] = p[OFF[j + 1] : OFF[j + 1] + n, :] - both[128:, 128:]
                j += 2
        p[o + 128 : o + 128 + m, :] = gain

    lax.fori_loop(0, NB, panel, 0)
    u = [None] * NB
    for k in reversed(range(NB)):
        o = OFF[k]
        m = (NB - 1 - k) * 128
        acc = p[o + 128 + m : o + 128 + m + PAD, :]
        if k < NB - 1:
            done = jnp.concatenate(u[k + 1 :], axis=1)
            acc = acc - lax.dot_general(
                done,
                p[o + 128 : o + 128 + m, :],
                NN,
                precision=lax.Precision.HIGHEST,
                preferred_element_type=f32,
            )
        u[k] = acc
        us[k] = acc
    full = jnp.concatenate(u, axis=1)
    uh, ul = split2(full)
    new_weights[...] = weights[...] + us[meta[0]][:C]
    for c in later:
        c.wait()
    fit = dot(uh, fh[...], NN) + dot(uh, fl[...], NN) + dot(ul, fh[...], NN)
    new_residual[...] = residual[...] - fit[:C]


def x_perm(s):
    return [(f, ((f // 2 + s) % 4) * 2 + f % 2) for f in range(8)]


BOTH = ("feat", "rows")


def device_of(x, y, z, c):
    return (2 * x + c) * 32 + 8 * y + z


def ring_perm(s):
    pairs = []
    for x in range(4):
        for y in range(4):
            for z in range(8):
                pairs.append((device_of(x, y, z, 0), device_of((x + s) % 4, y, z, 0)))
                pairs.append((device_of(x, y, z, 1), device_of(x, (y + s) % 4, z, 1)))
    return pairs


GROUPS = [[device_of(x, y, z, 0) for y in range(4) for z in range(8)] for x in range(4)] + [
    [device_of(x, y, z, 1) for x in range(4) for z in range(8)] for y in range(4)
]

core_swap = [(f, f ^ 1) for f in range(8)]


def per_device(samples, residual, bank, bank_phase, bank_weights, block_index):
    chosen = block_index[0]
    feat = lax.axis_index("feat")
    rows = lax.axis_index("rows")
    x, core = feat // 2, feat % 2
    y = rows // 8
    block = jnp.concatenate(
        [
            lax.dynamic_index_in_dim(bank, chosen, 0, keepdims=False),
            lax.dynamic_index_in_dim(bank_phase, chosen, 0, keepdims=True),
            jnp.zeros((7, 128), f32),
        ],
        axis=0,
    )
    local_weights = lax.dynamic_index_in_dim(bank_weights, chosen, 0, keepdims=False)
    mine = jnp.stack([block] + [lax.ppermute(block, "feat", x_perm(s)) for s in (1, 2, 3)])
    order = [
        (x + 4 - f // 2) % 4 + jnp.where(core == f % 2, 0, 4) for f in range(8)
    ]
    meta = jnp.stack(order + [jnp.where(rows == 0, feat, -1), core]).astype(jnp.int32)
    mine, meta, local_weights = lax.optimization_barrier((mine, meta, local_weights))
    theirs = lax.ppermute(mine, "feat", core_swap)
    smem = pl.BlockSpec(memory_space=pltpu.SMEM)
    vmem = pl.BlockSpec(memory_space=pltpu.VMEM)
    hbm = pl.BlockSpec(memory_space=pl.ANY)
    keep, give, fh, fl = pl.pallas_call(
        gram_kernel,
        out_shape=(
            jax.ShapeDtypeStruct((HALF, 128), f32),
            jax.ShapeDtypeStruct((HALF, 128), f32),
            jax.ShapeDtypeStruct((FB, COLS), bf16),
            jax.ShapeDtypeStruct((FB, COLS), bf16),
        ),
        in_specs=[smem, hbm, hbm, hbm, hbm, hbm],
        out_specs=(hbm, hbm, hbm, hbm),
        scratch_shapes=[
            pltpu.VMEM((8, 448, 128), f32),
            pltpu.VMEM((D, COLS), f32),
            pltpu.VMEM((C, COLS), f32),
            pltpu.VMEM((C, 128), f32),
            pltpu.VMEM((2, HALF, 128), f32),
            pltpu.VMEM((FB, COLS), bf16),
            pltpu.VMEM((FB, COLS), bf16),
            pltpu.SemaphoreType.DMA((5,)),
        ],
        compiler_params=pltpu.CompilerParams(vmem_limit_bytes=56 << 20),
        name="features_gram",
    )(meta, mine, theirs, samples, residual, local_weights)

    spot = jnp.where(core == 0, x, y)
    half = keep + lax.ppermute(give, "feat", core_swap)
    quarters = half.reshape(4, QUART, 128)
    got = [
        lax.ppermute(
            lax.dynamic_index_in_dim(quarters, (spot + s) % 4, 0, keepdims=False), BOTH, ring_perm(s)
        )
        for s in (1, 2, 3)
    ]
    quarter = lax.dynamic_index_in_dim(quarters, spot, 0, keepdims=False) + got[0] + got[1] + got[2]
    spread = jnp.pad(quarter, ((0, 32 * CHUNK - QUART), (0, 0))).reshape(32, CHUNK, 128)
    chunk = jnp.sum(lax.all_to_all(spread, BOTH, 0, 0, axis_index_groups=GROUPS), axis=0)
    full = lax.all_to_all(
        jnp.broadcast_to(chunk[None], (32, CHUNK, 128)), BOTH, 0, 0, axis_index_groups=GROUPS
    )
    quarter = full.reshape(32 * CHUNK, 128)[:QUART]
    own = jnp.stack([quarter] + [lax.ppermute(quarter, BOTH, ring_perm(s)) for s in (1, 2, 3)])
    other = lax.ppermute(own, "feat", core_swap)

    where = jnp.stack([feat, core, spot, jnp.where(core == 0, y, x)]).astype(jnp.int32)
    new_weights, new_residual = pl.pallas_call(
        solve_kernel,
        out_shape=(
            jax.ShapeDtypeStruct((C, 128), f32),
            jax.ShapeDtypeStruct((C, COLS), f32),
        ),
        in_specs=[smem, hbm, hbm, hbm, hbm, vmem, vmem],
        out_specs=(vmem, vmem),
        scratch_shapes=[
            pltpu.VMEM((T, 128), f32),
            pltpu.VMEM((128, 128), f32),
            pltpu.VMEM((NB, PAD, 128), f32),
            pltpu.VMEM((FB, COLS), bf16),
            pltpu.VMEM((FB, COLS), bf16),
            pltpu.SemaphoreType.DMA,
            pltpu.SemaphoreType.DMA,
        ],
        compiler_params=pltpu.CompilerParams(vmem_limit_bytes=56 << 20),
        name="block_solve",
    )(where, own, other, fh, fl, residual, local_weights)
    return (new_weights, new_residual)


def solution(mesh):
    in_specs = (
        P(None, ("feat", "rows")),
        P(None, ("feat", "rows")),
        P(None, None, "feat"),
        P(None, "feat"),
        P(None, None, "feat"),
        P(),
    )
    out_specs = (P(None, "feat"), P(None, ("feat", "rows")))
    return jax.shard_map(
        per_device, mesh=mesh, in_specs=in_specs, out_specs=out_specs, check_vma=False
    )
```

```python
import jax
import jax.numpy as jnp
from jax import lax
from jax.experimental import pallas as pl
from jax.experimental.pallas import tpu as pltpu
from jax.sharding import PartitionSpec as P


ridge_weight = 0.05
D = 440
C = 147
FB = 1024
NB = 8
PAD = 152
COLS = 1024
OFF = [0]
for _k in range(NB):
    OFF.append(OFF[-1] + (NB - _k) * 128 + PAD)
T = OFF[-1]
HALF = T // 2
QUART = T // 8
CHUNK = 24
TURN = 0.15915494309189535
COS = (0.9999999890590223, -19.739204499453898, 64.93911745989527, -85.4501395308797, 60.167630950920234, -25.967599248327534, 6.528658161042403)
f32 = jnp.float32
bf16 = jnp.bfloat16
NN = (((1,), (0,)), ((), ()))
NT = (((1,), (1,)), ((), ()))


def dot(l, r, dims):
    return lax.dot_general(l, r, dims, preferred_element_type=f32)


def split2(x):
    a = x.astype(bf16)
    return a, (x - a.astype(f32)).astype(bf16)


def split3(x):
    a = x.astype(bf16)
    r = x - a.astype(f32)
    b = r.astype(bf16)
    return a, b, (r - b.astype(f32)).astype(bf16)


def gram_kernel(
    meta, mine, theirs, samples_in, residual_in, weights_in, keep, give, fh_out, fl_out,
    proj, samples, residual, weights, packed, fh, fl, sem,
):
    first = pltpu.make_async_copy(samples_in, samples, sem.at[0])
    blocks = [
        pltpu.make_async_copy(mine, proj.at[0:4], sem.at[1]),
        pltpu.make_async_copy(theirs, proj.at[4:8], sem.at[2]),
    ]
    rest = [
        pltpu.make_async_copy(residual_in, residual, sem.at[3]),
        pltpu.make_async_copy(weights_in, weights, sem.at[4]),
    ]
    for c in [first] + blocks + rest:
        c.start()
    first.wait()
    s = jnp.concatenate([samples[...], jnp.zeros((8, COLS), f32)], axis=0)
    sh, sl = split2(s)
    for c in blocks:
        c.wait()
    for f in range(8):
        turned = (proj[meta[f]] * TURN).T
        h, l = split2(turned)
        y = dot(h, sh, NN) + dot(h, sl, NN) + dot(l, sh, NN) + turned[:, D : D + 1]
        r = y - jnp.round(y)
        z = r * r
        c = jnp.full_like(z, COS[-1])
        for a in COS[-2::-1]:
            c = c * z + a
        ch, cl = split2(c)
        fh[128 * f : 128 * f + 128, :] = ch
        fl[128 * f : 128 * f + 128, :] = cl
    out = [
        pltpu.make_async_copy(fh, fh_out, sem.at[0]),
        pltpu.make_async_copy(fl, fl_out, sem.at[1]),
    ]
    for c in out:
        c.start()
    for c in rest:
        c.wait()
    rh, rl = split2(jnp.concatenate([residual[...], jnp.zeros((PAD - C, COLS), f32)], axis=0))
    inv = 1.0 / (COLS * 256)

    def put(at, value):
        n = value.shape[0]
        low = min(max(HALF - at, 0), n)
        if low > 0:
            packed[meta[9], at : at + low, :] = value[:low]
        if low < n:
            packed[1 - meta[9], at + low - HALF : at + n - HALF, :] = value[low:]

    ridge = jnp.concatenate([weights[...], jnp.zeros((PAD - C, 128), f32)], axis=0) * (-ridge_weight)
    for q in range(4):
        o = 256 * q
        ch, cl = fh[o : o + 256, :], fl[o : o + 256, :]
        g = (dot(fh[o:, :], ch, NT) + dot(fh[o:, :], cl, NT) + dot(fl[o:, :], ch, NT)) * inv
        r = (dot(rh, ch, NT) + dot(rh, cl, NT) + dot(rl, ch, NT)) * inv
        for j in range(2):
            k = 2 * q + j
            m = (NB - k) * 128
            put(OFF[k], g[128 * j :, 128 * j : 128 * j + 128])
            own = jnp.where(meta[8] == k, 1.0, 0.0)
            put(OFF[k] + m, r[:, 128 * j : 128 * j + 128] + ridge * own)
    out = out + [
        pltpu.make_async_copy(packed.at[1], give, sem.at[2]),
        pltpu.make_async_copy(packed.at[0], keep, sem.at[3]),
    ]
    for c in out[2:]:
        c.start()
    for c in out:
        c.wait()


def tree(xs):
    xs = list(xs)
    while len(xs) > 1:
        last = [xs[-1]] if len(xs) % 2 else []
        xs = [xs[i] + xs[i + 1] for i in range(0, len(xs) - 1, 2)] + last
    return xs[0]


def sweep_slab(rows, lane, sub):
    d = list(rows)
    n = len(d)
    for g in range(n):
        c0 = 8 * g
        top = d[g]
        t = {}
        for j in range(8):
            cj = jnp.broadcast_to(top[:, c0 + j : c0 + j + 1], (8, 128))
            for i in range(j, 8):
                t[i, j] = jnp.take_along_axis(cj, jnp.full((8, 128), i, jnp.int32), axis=0)
        for p in range(0, 8, 2):
            q = p + 1
            e = 1.0 / (t[p, p] * t[q, q] - t[q, p] * t[q, p])
            epp, eqq, eqp = t[q, q] * e, t[p, p] * e, t[q, p] * e
            rest = [i for i in range(8) if i not in (p, q)]
            cp = {i: t[max(i, p), min(i, p)] for i in rest}
            cq = {i: t[max(i, q), min(i, q)] for i in rest}
            lp = {i: (cp[i] * t[q, q] - cq[i] * t[q, p]) * e for i in rest}
            lq = {i: (cq[i] * t[p, p] - cp[i] * t[q, p]) * e for i in rest}
            for i in rest:
                for k in rest:
                    if k <= i:
                        t[i, k] = t[i, k] - (lp[i] * cp[k] + lq[i] * cq[k])
            for i in rest:
                t[max(i, p), min(i, p)] = lp[i]
                t[max(i, q), min(i, q)] = lq[i]
            t[p, p], t[q, q], t[q, p] = -epp, -eqq, eqp

        def column(j):
            e = [t[max(i, j), min(i, j)] for i in range(8)]
            even = (sub & 1) == 0
            e = [jnp.where(even, e[2 * i], e[2 * i + 1]) for i in range(4)]
            low = (sub & 2) == 0
            e = [jnp.where(low, e[0], e[1]), jnp.where(low, e[2], e[3])]
            return jnp.where(sub < 4, e[0], e[1])

        inside = (lane >= c0) & (lane < c0 + 8)
        unit = [
            jnp.where(
                inside,
                jnp.where(lane == c0 + j, 1.0, 0.0),
                jnp.broadcast_to(top[j : j + 1, :], (8, 128)),
            )
            for j in range(8)
        ]
        new = tree([column(j) * unit[j] for j in range(8)])
        spread = [jnp.broadcast_to(new[j : j + 1, :], (8, 128)) for j in range(8)]
        for i in list(range(g + 1, n)) + list(range(g)):
            old = d[i]
            d[i] = jnp.where(inside, 0.0, old) + tree(
                [jnp.broadcast_to(old[:, c0 + j : c0 + j + 1], (8, 128)) * spread[j] for j in range(8)]
            )
        d[g] = -new
    return d


def invert_block(d, lane, sub):
    wide = lax.broadcasted_iota(jnp.int32, (64, 128), 1)

    def body(s, carry):
        slab = sweep_slab([d[8 * i : 8 * i + 8, :] for i in range(8)], lane, sub)
        slab = jnp.concatenate(slab, axis=0)
        a, b, c = split3(jnp.concatenate([slab, jnp.zeros((64, 128), f32)], axis=0))
        rest = d[64:, :]
        rest = jnp.where(wide < 64, 0.0, rest) - dot(
            stack_left(rest), jnp.concatenate([a, b, a, c, a, b], axis=0), NN
        )
        d[:64, :] = pltpu.roll(rest, 64, 1)
        d[64:, :] = pltpu.roll(slab, 64, 1)
        return carry

    lax.fori_loop(0, 2, body, 0)


def stack_left(x):
    a, b, c = split3(x)
    return jnp.concatenate([a, a, b, a, c, b], axis=1)


def stack_right(x):
    a, b, c = split3(x)
    return jnp.concatenate([a, b, a, c, a, b], axis=1)


def solve_kernel(meta, own, other, fh_in, fl_in, residual, weights, new_weights, new_residual, p, dinv, us, fh, fl, sem, fsem):
    core = meta[1]
    pieces = []
    for side, src in enumerate((own, other)):
        half = core if side == 0 else 1 - core
        for s in range(4):
            row = half * HALF + ((meta[2 + side] + 4 - s) % 4) * QUART
            row = pl.multiple_of(row, 8)
            pieces.append(pltpu.make_async_copy(src.at[s], p.at[pl.ds(row, QUART)], sem))
    later = [pltpu.make_async_copy(fh_in, fh, fsem), pltpu.make_async_copy(fl_in, fl, fsem)]
    for c in pieces + later:
        c.start()
    for c in pieces:
        c.wait()
    lane = lax.broadcasted_iota(jnp.int32, (8, 128), 1)
    sub = lax.broadcasted_iota(jnp.int32, (8, 128), 0)
    eye = jnp.where(
        lax.broadcasted_iota(jnp.int32, (128, 128), 0) == lax.broadcasted_iota(jnp.int32, (128, 128), 1),
        ridge_weight,
        0.0,
    )

    def panel(k, carry):
        o = pl.multiple_of(k * (FB + PAD) - 64 * k * (k - 1), 8)
        dinv[...] = p[pl.ds(o, 128), :] + eye
        invert_block(dinv, lane, sub)
        for which in range(NB):
            pl.when(k == which)(lambda which=which: trailing(which))
        return carry

    def trailing(k):
        o = OFF[k]
        m = (NB - 1 - k) * 128 + PAD
        below = p[o + 128 : o + 128 + m, :]
        a, b, c = split3(below)
        da, db, dc = split3(dinv[...])
        zero = jnp.zeros((128, 128), bf16)
        wide = jnp.concatenate(
            [
                jnp.concatenate([da, da, da, zero], axis=1),
                jnp.concatenate([db, db, zero, dc], axis=1),
            ],
            axis=0,
        )
        gain = dot(jnp.concatenate([a, b, c, a], axis=1), wide, NT)
        gain = gain[:, :128] + gain[:, 128:]
        if k < NB - 1:
            left = stack_left(gain)
            right = stack_right(below[: m - PAD])
            j = k + 1
            if (NB - j) % 2:
                p[OFF[j] : OFF[j] + m, :] = p[OFF[j] : OFF[j] + m, :] - dot(left, right[:128], NT)
                j += 1
            while j < NB:
                b = (j - k - 1) * 128
                n = m - b
                both = dot(left[b:], right[b : b + 256], NT)
                p[OFF[j] : OFF[j] + n, :] = p[OFF[j] : OFF[j] + n, :] - both[:, :128]
                n -= 128
                p[OFF[j + 1] : OFF[j + 1] + n, :] = p[OFF[j + 1] : OFF[j + 1] + n, :] - both[128:, 128:]
                j += 2
        p[o + 128 : o + 128 + m, :] = gain

    lax.fori_loop(0, NB, panel, 0)
    u = [None] * NB
    for k in reversed(range(NB)):
        o = OFF[k]
        m = (NB - 1 - k) * 128
        acc = p[o + 128 + m : o + 128 + m + PAD, :]
        if k < NB - 1:
            done = jnp.concatenate(u[k + 1 :], axis=1)
            acc = acc - lax.dot_general(
                done,
                p[o + 128 : o + 128 + m, :],
                NN,
                precision=lax.Precision.HIGHEST,
                preferred_element_type=f32,
            )
        u[k] = acc
        us[k] = acc
    full = jnp.concatenate(u, axis=1)
    uh, ul = split2(full)
    new_weights[...] = weights[...] + us[meta[0]][:C]
    for c in later:
        c.wait()
    fit = dot(uh, fh[...], NN) + dot(uh, fl[...], NN) + dot(ul, fh[...], NN)
    new_residual[...] = residual[...] - fit[:C]


def x_perm(s):
    return [(f, ((f // 2 + s) % 4) * 2 + f % 2) for f in range(8)]


BOTH = ("feat", "rows")


def device_of(x, y, z, c):
    return (2 * x + c) * 32 + 8 * y + z


def ring_perm(s):
    pairs = []
    for x in range(4):
        for y in range(4):
            for z in range(8):
                pairs.append((device_of(x, y, z, 0), device_of((x + s) % 4, y, z, 0)))
                pairs.append((device_of(x, y, z, 1), device_of(x, (y + s) % 4, z, 1)))
    return pairs


GROUPS = [[device_of(x, y, z, 0) for y in range(4) for z in range(8)] for x in range(4)] + [
    [device_of(x, y, z, 1) for x in range(4) for z in range(8)] for y in range(4)
]

core_swap = [(f, f ^ 1) for f in range(8)]


def shifted(perm, axis, values):
    got = {}
    for s in (2, 1, 3):
        got[s] = lax.ppermute(values[s], axis, perm(s))
    return [got[s] for s in (1, 2, 3)]


def per_device(samples, residual, bank, bank_phase, bank_weights, block_index):
    chosen = block_index[0]
    feat = lax.axis_index("feat")
    rows = lax.axis_index("rows")
    x, core = feat // 2, feat % 2
    y = rows // 8
    block = jnp.concatenate(
        [
            lax.dynamic_index_in_dim(bank, chosen, 0, keepdims=False),
            lax.dynamic_index_in_dim(bank_phase, chosen, 0, keepdims=True),
            jnp.zeros((7, 128), f32),
        ],
        axis=0,
    )
    local_weights = lax.dynamic_index_in_dim(bank_weights, chosen, 0, keepdims=False)
    mine = jnp.stack([block] + shifted(x_perm, "feat", [block] * 4))
    order = [
        (x + 4 - f // 2) % 4 + jnp.where(core == f % 2, 0, 4) for f in range(8)
    ]
    meta = jnp.stack(order + [jnp.where(rows == 0, feat, -1), core]).astype(jnp.int32)
    mine, meta, local_weights = lax.optimization_barrier((mine, meta, local_weights))
    theirs = lax.ppermute(mine, "feat", core_swap)
    smem = pl.BlockSpec(memory_space=pltpu.SMEM)
    vmem = pl.BlockSpec(memory_space=pltpu.VMEM)
    hbm = pl.BlockSpec(memory_space=pl.ANY)
    keep, give, fh, fl = pl.pallas_call(
        gram_kernel,
        out_shape=(
            jax.ShapeDtypeStruct((HALF, 128), f32),
            jax.ShapeDtypeStruct((HALF, 128), f32),
            jax.ShapeDtypeStruct((FB, COLS), bf16),
            jax.ShapeDtypeStruct((FB, COLS), bf16),
        ),
        in_specs=[smem, hbm, hbm, hbm, hbm, hbm],
        out_specs=(hbm, hbm, hbm, hbm),
        scratch_shapes=[
            pltpu.VMEM((8, 448, 128), f32),
            pltpu.VMEM((D, COLS), f32),
            pltpu.VMEM((C, COLS), f32),
            pltpu.VMEM((C, 128), f32),
            pltpu.VMEM((2, HALF, 128), f32),
            pltpu.VMEM((FB, COLS), bf16),
            pltpu.VMEM((FB, COLS), bf16),
            pltpu.SemaphoreType.DMA((5,)),
        ],
        compiler_params=pltpu.CompilerParams(vmem_limit_bytes=56 << 20),
        name="features_gram",
    )(meta, mine, theirs, samples, residual, local_weights)

    spot = jnp.where(core == 0, x, y)
    half = keep + lax.ppermute(give, "feat", core_swap)
    quarters = half.reshape(4, QUART, 128)
    leaving = [
        lax.dynamic_index_in_dim(quarters, (spot + s) % 4, 0, keepdims=False) for s in range(4)
    ]
    got = shifted(ring_perm, BOTH, leaving)
    quarter = leaving[0] + got[0] + got[1] + got[2]
    spread = jnp.pad(quarter, ((0, 32 * CHUNK - QUART), (0, 0))).reshape(32, CHUNK, 128)
    chunk = jnp.sum(lax.all_to_all(spread, BOTH, 0, 0, axis_index_groups=GROUPS), axis=0)
    full = lax.all_to_all(
        jnp.broadcast_to(chunk[None], (32, CHUNK, 128)), BOTH, 0, 0, axis_index_groups=GROUPS
    )
    quarter = full.reshape(32 * CHUNK, 128)[:QUART]
    own = jnp.stack([quarter] + shifted(ring_perm, BOTH, [quarter] * 4))
    other = lax.ppermute(own, "feat", core_swap)

    where = jnp.stack([feat, core, spot, jnp.where(core == 0, y, x)]).astype(jnp.int32)
    new_weights, new_residual = pl.pallas_call(
        solve_kernel,
        out_shape=(
            jax.ShapeDtypeStruct((C, 128), f32),
            jax.ShapeDtypeStruct((C, COLS), f32),
        ),
        in_specs=[smem, hbm, hbm, hbm, hbm, vmem, vmem],
        out_specs=(vmem, vmem),
        scratch_shapes=[
            pltpu.VMEM((T, 128), f32),
            pltpu.VMEM((128, 128), f32),
            pltpu.VMEM((NB, PAD, 128), f32),
            pltpu.VMEM((FB, COLS), bf16),
            pltpu.VMEM((FB, COLS), bf16),
            pltpu.SemaphoreType.DMA,
            pltpu.SemaphoreType.DMA,
        ],
        compiler_params=pltpu.CompilerParams(vmem_limit_bytes=56 << 20),
        name="block_solve",
    )(where, own, other, fh, fl, residual, local_weights)
    return (new_weights, new_residual)


def solution(mesh):
    in_specs = (
        P(None, ("feat", "rows")),
        P(None, ("feat", "rows")),
        P(None, None, "feat"),
        P(None, "feat"),
        P(None, None, "feat"),
        P(),
    )
    out_specs = (P(None, "feat"), P(None, ("feat", "rows")))
    return jax.shard_map(
        per_device, mesh=mesh, in_specs=in_specs, out_specs=out_specs, check_vma=False
    )
```

```python
import jax
import jax.numpy as jnp
from jax import lax
from jax.experimental import pallas as pl
from jax.experimental.pallas import tpu as pltpu
from jax.sharding import PartitionSpec as P


ridge_weight = 0.05
D = 440
C = 147
FB = 1024
NB = 8
PAD = 152
COLS = 1024
OFF = [0]
for _k in range(NB):
    OFF.append(OFF[-1] + (NB - _k) * 128 + PAD)
T = OFF[-1]
HALF = T // 2
QUART = T // 8
CHUNK = 24
TURN = 0.15915494309189535
COS = (0.9999999890590223, -19.739204499453898, 64.93911745989527, -85.4501395308797, 60.167630950920234, -25.967599248327534, 6.528658161042403)
f32 = jnp.float32
bf16 = jnp.bfloat16
NN = (((1,), (0,)), ((), ()))
NT = (((1,), (1,)), ((), ()))


def dot(l, r, dims):
    return lax.dot_general(l, r, dims, preferred_element_type=f32)


def split2(x):
    a = x.astype(bf16)
    return a, (x - a.astype(f32)).astype(bf16)


def split3(x):
    a = x.astype(bf16)
    r = x - a.astype(f32)
    b = r.astype(bf16)
    return a, b, (r - b.astype(f32)).astype(bf16)


def gram_kernel(
    meta, mine, theirs, samples_in, residual_in, weights_in, keep, give, fh_out, fl_out,
    proj, samples, residual, weights, packed, fh, fl, sem,
):
    first = pltpu.make_async_copy(samples_in, samples, sem.at[0])
    blocks = [
        pltpu.make_async_copy(mine, proj.at[0:4], sem.at[1]),
        pltpu.make_async_copy(theirs, proj.at[4:8], sem.at[2]),
    ]
    rest = [
        pltpu.make_async_copy(residual_in, residual, sem.at[3]),
        pltpu.make_async_copy(weights_in, weights, sem.at[4]),
    ]
    for c in [first] + blocks + rest:
        c.start()
    first.wait()
    s = jnp.concatenate([samples[...], jnp.zeros((8, COLS), f32)], axis=0)
    sh, sl = split2(s)
    for c in blocks:
        c.wait()
    for f in range(8):
        turned = (proj[meta[f]] * TURN).T
        h, l = split2(turned)
        y = dot(h, sh, NN) + dot(h, sl, NN) + dot(l, sh, NN) + turned[:, D : D + 1]
        r = y - jnp.round(y)
        z = r * r
        c = jnp.full_like(z, COS[-1])
        for a in COS[-2::-1]:
            c = c * z + a
        ch, cl = split2(c)
        fh[128 * f : 128 * f + 128, :] = ch
        fl[128 * f : 128 * f + 128, :] = cl
    out = [
        pltpu.make_async_copy(fh, fh_out, sem.at[0]),
        pltpu.make_async_copy(fl, fl_out, sem.at[1]),
    ]
    for c in out:
        c.start()
    for c in rest:
        c.wait()
    rh, rl = split2(jnp.concatenate([residual[...], jnp.zeros((PAD - C, COLS), f32)], axis=0))
    inv = 1.0 / (COLS * 256)

    def put(at, value):
        n = value.shape[0]
        low = min(max(HALF - at, 0), n)
        if low > 0:
            packed[meta[9], at : at + low, :] = value[:low]
        if low < n:
            packed[1 - meta[9], at + low - HALF : at + n - HALF, :] = value[low:]

    ridge = jnp.concatenate([weights[...], jnp.zeros((PAD - C, 128), f32)], axis=0) * (-ridge_weight)
    for q in range(4):
        o = 256 * q
        ch, cl = fh[o : o + 256, :], fl[o : o + 256, :]
        g = (dot(fh[o:, :], ch, NT) + dot(fh[o:, :], cl, NT) + dot(fl[o:, :], ch, NT)) * inv
        r = (dot(rh, ch, NT) + dot(rh, cl, NT) + dot(rl, ch, NT)) * inv
        for j in range(2):
            k = 2 * q + j
            m = (NB - k) * 128
            put(OFF[k], g[128 * j :, 128 * j : 128 * j + 128])
            own = jnp.where(meta[8] == k, 1.0, 0.0)
            put(OFF[k] + m, r[:, 128 * j : 128 * j + 128] + ridge * own)
    out = out + [
        pltpu.make_async_copy(packed.at[1], give, sem.at[2]),
        pltpu.make_async_copy(packed.at[0], keep, sem.at[3]),
    ]
    for c in out[2:]:
        c.start()
    for c in out:
        c.wait()


def tree(xs):
    xs = list(xs)
    while len(xs) > 1:
        last = [xs[-1]] if len(xs) % 2 else []
        xs = [xs[i] + xs[i + 1] for i in range(0, len(xs) - 1, 2)] + last
    return xs[0]


def sweep_slab(rows, lane, sub):
    d = list(rows)
    n = len(d)
    for g in range(n):
        c0 = 8 * g
        top = d[g]
        t = {}
        for j in range(8):
            cj = jnp.broadcast_to(top[:, c0 + j : c0 + j + 1], (8, 128))
            for i in range(j, 8):
                t[i, j] = jnp.take_along_axis(cj, jnp.full((8, 128), i, jnp.int32), axis=0)
        for p in range(0, 8, 2):
            q = p + 1
            e = 1.0 / (t[p, p] * t[q, q] - t[q, p] * t[q, p])
            epp, eqq, eqp = t[q, q] * e, t[p, p] * e, t[q, p] * e
            rest = [i for i in range(8) if i not in (p, q)]
            cp = {i: t[max(i, p), min(i, p)] for i in rest}
            cq = {i: t[max(i, q), min(i, q)] for i in rest}
            lp = {i: (cp[i] * t[q, q] - cq[i] * t[q, p]) * e for i in rest}
            lq = {i: (cq[i] * t[p, p] - cp[i] * t[q, p]) * e for i in rest}
            for i in rest:
                for k in rest:
                    if k <= i:
                        t[i, k] = t[i, k] - (lp[i] * cp[k] + lq[i] * cq[k])
            for i in rest:
                t[max(i, p), min(i, p)] = lp[i]
                t[max(i, q), min(i, q)] = lq[i]
            t[p, p], t[q, q], t[q, p] = -epp, -eqq, eqp

        def column(j):
            e = [t[max(i, j), min(i, j)] for i in range(8)]
            even = (sub & 1) == 0
            e = [jnp.where(even, e[2 * i], e[2 * i + 1]) for i in range(4)]
            low = (sub & 2) == 0
            e = [jnp.where(low, e[0], e[1]), jnp.where(low, e[2], e[3])]
            return jnp.where(sub < 4, e[0], e[1])

        inside = (lane >= c0) & (lane < c0 + 8)
        unit = [
            jnp.where(
                inside,
                jnp.where(lane == c0 + j, 1.0, 0.0),
                jnp.broadcast_to(top[j : j + 1, :], (8, 128)),
            )
            for j in range(8)
        ]
        new = tree([column(j) * unit[j] for j in range(8)])
        spread = [jnp.broadcast_to(new[j : j + 1, :], (8, 128)) for j in range(8)]
        for i in list(range(g + 1, n)) + list(range(g)):
            old = d[i]
            d[i] = jnp.where(inside, 0.0, old) + tree(
                [jnp.broadcast_to(old[:, c0 + j : c0 + j + 1], (8, 128)) * spread[j] for j in range(8)]
            )
        d[g] = -new
    return d


def invert_block(d, lane, sub):
    wide = lax.broadcasted_iota(jnp.int32, (64, 128), 1)

    def body(s, carry):
        slab = sweep_slab([d[8 * i : 8 * i + 8, :] for i in range(8)], lane, sub)
        slab = jnp.concatenate(slab, axis=0)
        a, b, c = split3(jnp.concatenate([slab, jnp.zeros((64, 128), f32)], axis=0))
        rest = d[64:, :]
        rest = jnp.where(wide < 64, 0.0, rest) - dot(
            stack_left(rest), jnp.concatenate([a, b, a, c, a, b], axis=0), NN
        )
        d[:64, :] = pltpu.roll(rest, 64, 1)
        d[64:, :] = pltpu.roll(slab, 64, 1)
        return carry

    lax.fori_loop(0, 2, body, 0)


def stack_left(x):
    a, b, c = split3(x)
    return jnp.concatenate([a, a, b, a, c, b], axis=1)


def solve_kernel(meta, own, other, fh_in, fl_in, residual, weights, new_weights, new_residual, p, dinv, us, fh, fl, sem, fsem):
    core = meta[1]
    pieces = []
    for side, src in enumerate((own, other)):
        half = core if side == 0 else 1 - core
        for s in range(4):
            row = half * HALF + ((meta[2 + side] + 4 - s) % 4) * QUART
            row = pl.multiple_of(row, 8)
            pieces.append(pltpu.make_async_copy(src.at[s], p.at[pl.ds(row, QUART)], sem))
    later = [pltpu.make_async_copy(fh_in, fh, fsem), pltpu.make_async_copy(fl_in, fl, fsem)]
    for c in pieces + later:
        c.start()
    for c in pieces:
        c.wait()
    lane = lax.broadcasted_iota(jnp.int32, (8, 128), 1)
    sub = lax.broadcasted_iota(jnp.int32, (8, 128), 0)
    eye = jnp.where(
        lax.broadcasted_iota(jnp.int32, (128, 128), 0) == lax.broadcasted_iota(jnp.int32, (128, 128), 1),
        ridge_weight,
        0.0,
    )

    def panel(k, carry):
        o = pl.multiple_of(k * (FB + PAD) - 64 * k * (k - 1), 8)
        dinv[...] = p[pl.ds(o, 128), :] + eye
        invert_block(dinv, lane, sub)
        for which in range(NB):
            pl.when(k == which)(lambda which=which: trailing(which))
        return carry

    def trailing(k):
        o = OFF[k]
        m = (NB - 1 - k) * 128 + PAD
        below = p[o + 128 : o + 128 + m, :]
        a, b, c = split3(below)
        da, db, dc = split3(dinv[...])
        zero = jnp.zeros((128, 128), bf16)
        wide = jnp.concatenate(
            [
                jnp.concatenate([da, da, da, zero], axis=1),
                jnp.concatenate([db, db, zero, dc], axis=1),
            ],
            axis=0,
        )
        gain = dot(jnp.concatenate([a, b, c, a], axis=1), wide, NT)
        gain = gain[:, :128] + gain[:, 128:]
        if k < NB - 1:
            left = stack_left(gain)
            right = jnp.concatenate([a, b, a, c, a, b], axis=1)[: m - PAD]
            j = k + 1
            if (NB - j) % 2:
                p[OFF[j] : OFF[j] + m, :] = p[OFF[j] : OFF[j] + m, :] - dot(left, right[:128], NT)
                j += 1
            while j < NB:
                skip = (j - k - 1) * 128
                n = m - skip
                both = dot(left[skip:], right[skip : skip + 256], NT)
                p[OFF[j] : OFF[j] + n, :] = p[OFF[j] : OFF[j] + n, :] - both[:, :128]
                n -= 128
                p[OFF[j + 1] : OFF[j + 1] + n, :] = p[OFF[j + 1] : OFF[j + 1] + n, :] - both[128:, 128:]
                j += 2
        p[o + 128 : o + 128 + m, :] = gain

    lax.fori_loop(0, NB, panel, 0)
    u = [None] * NB
    for k in reversed(range(NB)):
        o = OFF[k]
        m = (NB - 1 - k) * 128
        acc = p[o + 128 + m : o + 128 + m + PAD, :]
        if k < NB - 1:
            done = jnp.concatenate(u[k + 1 :], axis=1)
            acc = acc - lax.dot_general(
                done,
                p[o + 128 : o + 128 + m, :],
                NN,
                precision=lax.Precision.HIGHEST,
                preferred_element_type=f32,
            )
        u[k] = acc
        us[k] = acc
    full = jnp.concatenate(u, axis=1)
    uh, ul = split2(full)
    new_weights[...] = weights[...] + us[meta[0]][:C]
    for c in later:
        c.wait()
    fit = dot(uh, fh[...], NN) + dot(uh, fl[...], NN) + dot(ul, fh[...], NN)
    new_residual[...] = residual[...] - fit[:C]


def x_perm(s):
    return [(f, ((f // 2 + s) % 4) * 2 + f % 2) for f in range(8)]


BOTH = ("feat", "rows")


def device_of(x, y, z, c):
    return (2 * x + c) * 32 + 8 * y + z


def ring_perm(s):
    pairs = []
    for x in range(4):
        for y in range(4):
            for z in range(8):
                pairs.append((device_of(x, y, z, 0), device_of((x + s) % 4, y, z, 0)))
                pairs.append((device_of(x, y, z, 1), device_of(x, (y + s) % 4, z, 1)))
    return pairs


GROUPS = [[device_of(x, y, z, 0) for y in range(4) for z in range(8)] for x in range(4)] + [
    [device_of(x, y, z, 1) for x in range(4) for z in range(8)] for y in range(4)
]

core_swap = [(f, f ^ 1) for f in range(8)]


def shifted(perm, axis, values):
    got = {}
    for s in (2, 1, 3):
        got[s] = lax.ppermute(values[s], axis, perm(s))
    return [got[s] for s in (1, 2, 3)]


def per_device(samples, residual, bank, bank_phase, bank_weights, block_index):
    chosen = block_index[0]
    feat = lax.axis_index("feat")
    rows = lax.axis_index("rows")
    x, core = feat // 2, feat % 2
    y = rows // 8
    block = jnp.concatenate(
        [
            lax.dynamic_index_in_dim(bank, chosen, 0, keepdims=False),
            lax.dynamic_index_in_dim(bank_phase, chosen, 0, keepdims=True),
            jnp.zeros((7, 128), f32),
        ],
        axis=0,
    )
    local_weights = lax.dynamic_index_in_dim(bank_weights, chosen, 0, keepdims=False)
    mine = jnp.stack([block] + shifted(x_perm, "feat", [block] * 4))
    order = [
        (x + 4 - f // 2) % 4 + jnp.where(core == f % 2, 0, 4) for f in range(8)
    ]
    meta = jnp.stack(order + [jnp.where(rows == 0, feat, -1), core]).astype(jnp.int32)
    mine, meta, local_weights = lax.optimization_barrier((mine, meta, local_weights))
    theirs = lax.ppermute(mine, "feat", core_swap)
    smem = pl.BlockSpec(memory_space=pltpu.SMEM)
    vmem = pl.BlockSpec(memory_space=pltpu.VMEM)
    hbm = pl.BlockSpec(memory_space=pl.ANY)
    keep, give, fh, fl = pl.pallas_call(
        gram_kernel,
        out_shape=(
            jax.ShapeDtypeStruct((HALF, 128), f32),
            jax.ShapeDtypeStruct((HALF, 128), f32),
            jax.ShapeDtypeStruct((FB, COLS), bf16),
            jax.ShapeDtypeStruct((FB, COLS), bf16),
        ),
        in_specs=[smem, hbm, hbm, hbm, hbm, hbm],
        out_specs=(hbm, hbm, hbm, hbm),
        scratch_shapes=[
            pltpu.VMEM((8, 448, 128), f32),
            pltpu.VMEM((D, COLS), f32),
            pltpu.VMEM((C, COLS), f32),
            pltpu.VMEM((C, 128), f32),
            pltpu.VMEM((2, HALF, 128), f32),
            pltpu.VMEM((FB, COLS), bf16),
            pltpu.VMEM((FB, COLS), bf16),
            pltpu.SemaphoreType.DMA((5,)),
        ],
        compiler_params=pltpu.CompilerParams(vmem_limit_bytes=56 << 20),
        name="features_gram",
    )(meta, mine, theirs, samples, residual, local_weights)

    spot = jnp.where(core == 0, x, y)
    received = lax.ppermute(give, "feat", core_swap)

    def leaving_quarter(s):
        at = (spot + s) % 4
        return lax.dynamic_index_in_dim(
            keep.reshape(4, QUART, 128), at, 0, keepdims=False
        ) + lax.dynamic_index_in_dim(received.reshape(4, QUART, 128), at, 0, keepdims=False)

    leaving = [leaving_quarter(s) for s in range(4)]
    got = shifted(ring_perm, BOTH, leaving)
    quarter = leaving[0] + got[0] + got[1] + got[2]
    spread = jnp.pad(quarter, ((0, 32 * CHUNK - QUART), (0, 0))).reshape(32, CHUNK, 128)
    chunk = jnp.sum(lax.all_to_all(spread, BOTH, 0, 0, axis_index_groups=GROUPS), axis=0)
    full = lax.all_to_all(
        jnp.broadcast_to(chunk[None], (32, CHUNK, 128)), BOTH, 0, 0, axis_index_groups=GROUPS
    )
    quarter = full.reshape(32 * CHUNK, 128)[:QUART]
    own = jnp.stack([quarter] + shifted(ring_perm, BOTH, [quarter] * 4))
    other = lax.ppermute(own, "feat", core_swap)

    where = jnp.stack([feat, core, spot, jnp.where(core == 0, y, x)]).astype(jnp.int32)
    new_weights, new_residual = pl.pallas_call(
        solve_kernel,
        out_shape=(
            jax.ShapeDtypeStruct((C, 128), f32),
            jax.ShapeDtypeStruct((C, COLS), f32),
        ),
        in_specs=[smem, hbm, hbm, hbm, hbm, vmem, vmem],
        out_specs=(vmem, vmem),
        scratch_shapes=[
            pltpu.VMEM((T, 128), f32),
            pltpu.VMEM((128, 128), f32),
            pltpu.VMEM((NB, PAD, 128), f32),
            pltpu.VMEM((FB, COLS), bf16),
            pltpu.VMEM((FB, COLS), bf16),
            pltpu.SemaphoreType.DMA,
            pltpu.SemaphoreType.DMA,
        ],
        compiler_params=pltpu.CompilerParams(vmem_limit_bytes=56 << 20),
        name="block_solve",
    )(where, own, other, fh, fl, residual, local_weights)
    return (new_weights, new_residual)


def solution(mesh):
    in_specs = (
        P(None, ("feat", "rows")),
        P(None, ("feat", "rows")),
        P(None, None, "feat"),
        P(None, "feat"),
        P(None, None, "feat"),
        P(),
    )
    out_specs = (P(None, "feat"), P(None, ("feat", "rows")))
    return jax.shard_map(
        per_device, mesh=mesh, in_specs=in_specs, out_specs=out_specs, check_vma=False
    )
```
